32 devices in a mesh: space: 4 (over y, x), vel: 8 (over z, core).
Axes of the slice: x: 2, y: 2, z: 4, core: 2. Of those that a mesh axis runs over, the one named last changes fastest.
Arguments:
- cotangent: float32 [8192, 128, 128], P('vel', 'space'), may hold values from -6 to 6
- speed: float32 [3, 8192], P(None, 'vel'), may hold values from 0.1 to 3
- direction: int32 [3, 8192], P(None, 'vel'), may hold values from 0 to 1
- macroscopic_record: float32 [3, 5, 128, 128], P(None, None, 'space'), may hold values from -1 to 2, as said below
Outputs:
- gradient: float32 [8192, 128, 128], P('vel', 'space')
The draws below stay inside these ranges and needn't reach their ends.
Inputs may be any that keep to these rules, and one draw needn't show every extreme that they name: `direction`: 1 marks a positive velocity component, 0 a negative one. `macroscopic_record`: density and temperature lie between 0.5 and 2, flow velocity components between -1 and 1.
All inputs are finite; a program needn't handle non-finite values.
Results may differ from the reference program's by a relative error of at most 0.00013.
Values sent between devices are 32-bit elements; how exact they have to be, the bound alone decides.
No kernel may reach another device: no remote copies, remote signals or barrier semaphores. Data moves between devices by JAX's collectives and lax.ppermute only.
A program may use at most 128 MiB of HBM per device.

```python
import math
import jax
import jax.numpy as jnp
from jax import lax

SPEED_POINTS = 8192
NY = 128
STEPS = 3
NX = 128


def draw_macroscopic_record(key, part):
    key_density, key_flow, conduction_random_seed = jax.random.split(jax.random.fold_in(key, 71), 3)
    lattice_layout = (STEPS, NX, NY)
    particle_concentration = jnp.exp(jax.random.uniform(key_density, lattice_layout, jnp.float32, math.log(0.5), math.log(2.0)))
    thermal_energy_level = jnp.exp(jax.random.uniform(conduction_random_seed, lattice_layout, jnp.float32, math.log(0.5), math.log(2.0)))
    mean_drift = jnp.clip(0.3 * jax.random.normal(key_flow, (STEPS, 3, NX, NY), jnp.float32), -1.0, 1.0)
    return jnp.concatenate([particle_concentration[:, None], mean_drift, thermal_energy_level[:, None]], axis=1)


def place_ends(values, own_key, low, largest):
    dims = values.shape
    spot = [jax.random.randint(jax.random.fold_in(own_key, axis), (), 0, dims[axis]) for axis in range(len(dims))]
    values = values.at[tuple(spot)].set(low)
    longest = dims.index(max(dims))
    spot[longest] = (spot[longest] + 1) % dims[longest]
    return values.at[tuple(spot)].set(largest)


def shard_levels(stream_key, shape, pieces, smallest, top_value):
    def one(axis_at, shards_of):
        draws = jax.random.uniform(jax.random.fold_in(jax.random.fold_in(stream_key, 6), axis_at), (shards_of,), jnp.float32, smallest / len(pieces), top_value / len(pieces))
        return jnp.repeat(jnp.exp(draws), shape[axis_at] // shards_of).reshape((-1,) + (1,) * (len(shape) - axis_at - 1))

    level = one(*pieces[0])
    for cut in pieces[1:]:
        level = level * one(*cut)
    return level


def normal_values(rng, dims, scale, bound, shards=(), kind=jnp.bfloat16):
    result = jax.random.normal(rng, dims, jnp.float32) * scale
    if len(shards) > 0:
        result = shard_levels(rng, dims, shards, -0.22, 0.18) * result
    return jnp.clip(result, min=-bound, max=bound).astype(kind)


def setup_inputs(seed: int = 0) -> dict:
    seeds = jax.random.split(jax.random.key(seed), 5)
    return {
        "cotangent": normal_values(seeds[0], (SPEED_POINTS, NX, NY), 1.0, 6.0, ((0, 8), (1, 4)), jnp.float32),
        "speed": jnp.clip(0.1 + 2.9 * jax.random.uniform(seeds[1], (3, SPEED_POINTS), jnp.float32) ** shard_levels(seeds[1], (3, SPEED_POINTS), ((1, 8),), -0.2, 0.2), 0.1, 3.0),
        "direction": place_ends(jax.random.randint(seeds[2], (3, SPEED_POINTS), 0, 2), jax.random.fold_in(seeds[2], 1), 0, 1).astype(jnp.int32),
        "macroscopic_record": draw_macroscopic_record(jax.random.fold_in(seeds[4], 71), 0),
    }


courant_number = 0.1
region_capacity = 216.0
mode_gains = (1.0, 1.0, 1.0, 1.0, 1.0, -0.5, -0.5, -0.5, -0.5, -0.5, 1.0 / 3.0, 1.0 / 3.0, 1.0 / 3.0)

def hermite_modes(comp_x, comp_y, comp_z):
    square = comp_x * comp_x + comp_y * comp_y + comp_z * comp_z
    return [jnp.ones_like(comp_x), comp_x, comp_y, comp_z, (square - 3.0) / math.sqrt(6.0), comp_x * comp_y, comp_x * comp_z, comp_y * comp_z, (comp_x * comp_x - comp_y * comp_y) * 0.5, (comp_x * comp_x + comp_y * comp_y - 2.0 * comp_z * comp_z) / math.sqrt(12.0), comp_x * (square - 5.0) / math.sqrt(10.0), comp_y * (square - 5.0) / math.sqrt(10.0), comp_z * (square - 5.0) / math.sqrt(10.0)]

def pad_both(values, along):
    extent = values.shape[along]
    lower_rim = lax.slice_in_dim(values, extent - 2, extent, axis=along)
    upper_rim = lax.slice_in_dim(values, 0, 2, axis=along)
    return jnp.concatenate([lower_rim, values, upper_rim], axis=along)

def upwind_back(padded, length, along, lam_col, positive):

    def window(start_at):
        return lax.slice_in_dim(padded, start_at, start_at + length, axis=along)
    center = window(2)
    nearer = jnp.where(positive, window(3), window(1))
    farther = jnp.where(positive, window(4), window(0))
    return center - 0.5 * lam_col * (3.0 * center - 4.0 * nearer + farther)

def transport_back(adjoint, lam_x, lam_y, pos_x, pos_y):
    moved_y = upwind_back(pad_both(adjoint, 2), adjoint.shape[2], 2, lam_y, pos_y)
    return upwind_back(pad_both(moved_y, 1), adjoint.shape[1], 1, lam_x, pos_x)

def reference(cotangent, speed, direction, macroscopic_record):
    sign_values = (2 * direction - 1).astype(jnp.float32)
    velocity = sign_values * speed
    factors = courant_number * speed
    block_size = math.gcd(SPEED_POINTS, 512)
    count_blocks = SPEED_POINTS // block_size

    def blocked(array):
        return array.reshape((count_blocks, block_size) + array.shape[1:])
    vel_rows = blocked(velocity.T)
    lam_rows = blocked(factors.T)
    pos_rows = blocked(direction.T > 0)
    adjoint = cotangent
    for iteration_counter in range(STEPS - 1, -1, -1):
        particle_concentration = macroscopic_record[iteration_counter, 0]
        mean_drift = macroscopic_record[iteration_counter, 1:4]
        thermal_energy_level = macroscopic_record[iteration_counter, 4]
        reciprocal_factor = 1.0 / jnp.sqrt(thermal_energy_level)
        normalising_coefficient = particle_concentration * (2.0 * math.pi * thermal_energy_level) ** (-1.5) * region_capacity / SPEED_POINTS
        relaxation_rate = 0.3 * particle_concentration * jnp.sqrt(thermal_energy_level)

        def advect(inputs):
            field_blk, lam_blk, pos_blk = inputs
            return transport_back(field_blk, lam_blk[:, 0, None, None], lam_blk[:, 1, None, None], pos_blk[:, 0, None, None], pos_blk[:, 1, None, None])
        advected = lax.map(advect, (blocked(adjoint), lam_rows, pos_rows))

        def peculiar_of(vel_blk):
            return [(vel_blk[:, component, None, None] - mean_drift[component]) * reciprocal_factor for component in range(3)]

        def project(running, inputs):
            moved_blk, vel_blk = inputs
            peculiar = peculiar_of(vel_blk)
            weight = normalising_coefficient * jnp.exp(-0.5 * (peculiar[0] ** 2 + peculiar[1] ** 2 + peculiar[2] ** 2))
            weighted = weight * moved_blk
            mode_list = hermite_modes(peculiar[0], peculiar[1], peculiar[2])
            return (running + jnp.stack([lax.optimization_barrier(jnp.sum(mode_one * weighted, axis=0)) for mode_one in mode_list]), None)
        projection, unused = lax.scan(project, jnp.zeros((13, NX, NY), jnp.float32), (advected, vel_rows))
        weighted_proj = jnp.asarray(mode_gains, dtype=jnp.float32)[:, None, None] * projection

        def spread(inputs):
            moved_blk, vel_blk = inputs
            peculiar = peculiar_of(vel_blk)
            mode_list = hermite_modes(peculiar[0], peculiar[1], peculiar[2])
            returned = mode_list[0] * weighted_proj[0]
            for mode_place in range(1, 13):
                returned = returned + mode_list[mode_place] * weighted_proj[mode_place]
            return (1.0 - relaxation_rate) * moved_blk + relaxation_rate * returned
        adjoint = lax.map(spread, (advected, vel_rows)).reshape(SPEED_POINTS, NX, NY)
    return adjoint
```

```python
import functools
import math

import jax
import jax.numpy as jnp
from jax import lax
from jax.experimental import pallas as pl
from jax.experimental.pallas import tpu as pltpu
from jax.sharding import PartitionSpec as P


F32, BF16 = jnp.float32, jnp.bfloat16
COURANT = 0.1
REGION = 216.0
MODES = 13
GROUP = 16
LOG2E = math.log2(math.e)
VMEM_LIMIT = 60 * 1024 * 1024


def split3(x):
    high = x.astype(BF16)
    rest = x - high.astype(F32)
    middle = rest.astype(BF16)
    low = (rest - middle.astype(F32)).astype(BF16)
    return high, middle, low


def mxu(a, b):
    return jnp.dot(a, b, preferred_element_type=F32)


def tables_kernel(speed_ref, direction_ref, lhs_r, lhs_e, tab, cols, rows):
    count = speed_ref.shape[1]
    sign = (2 * direction_ref[...] - 1).astype(F32)
    speed = speed_ref[...]
    velocity = sign * speed
    vx, vy, vz = (velocity[k : k + 1] for k in range(3))
    square = vx * vx + vy * vy + vz * vz
    one = jnp.ones_like(vx)

    def put(values):
        rows[0:GROUP, :] = jnp.zeros((GROUP, count), F32)
        for place, value in enumerate(values):
            rows[place : place + 1, :] = value
        return split3(rows[0:GROUP, :])

    def left(parts):
        first, second, third = (part.astype(F32) for part in parts)
        for place, part in enumerate((first, first, second, second, first, third)):
            rows[place * GROUP : (place + 1) * GROUP, :] = part
        rows[6 * GROUP :, :] = jnp.zeros((rows.shape[0] - 6 * GROUP, count), F32)
        return rows[...].T.astype(BF16)

    parts = put(
        [one, vx, vy, vz, vx * vx, vy * vy, vz * vz, vx * vy, vx * vz, vy * vz]
        + [vx * square, vy * square, vz * square]
    )
    for place, part in enumerate(parts):
        tab[place * GROUP : (place + 1) * GROUP, :] = part
    lhs_r[...] = left(parts)
    lhs_e[...] = left(put([square, vx, vy, vz, one]))
    rows[...] = jnp.zeros_like(rows)
    for axis in range(2):
        lam = COURANT * speed[axis : axis + 1]
        rows[3 * axis : 3 * axis + 1, :] = 1.0 - 1.5 * lam
        rows[3 * axis + 1 : 3 * axis + 2, :] = 2.0 * lam
        rows[3 * axis + 2 : 3 * axis + 3, :] = -0.5 * lam
        rows[6 + axis : 7 + axis, :] = sign[axis : axis + 1]
    cols[...] = rows[...].T


def make_tables(speed, direction):
    count = speed.shape[1]
    return pl.pallas_call(
        tables_kernel,
        out_shape=(
            jax.ShapeDtypeStruct((count, 128), BF16),
            jax.ShapeDtypeStruct((count, 128), BF16),
            jax.ShapeDtypeStruct((3 * GROUP, count), BF16),
            jax.ShapeDtypeStruct((count, 128), F32),
        ),
        scratch_shapes=[pltpu.VMEM((128, count), F32)],
        name="tables",
    )(speed, direction)


def cell(macro, step, where):
    return [macro[step, pl.ds(k, 1), where] for k in range(5)]


def exponent_rows(macro, step, where, rhs, temp):
    _, ux, uy, uz, heat = cell(macro, step, where)
    inverse = LOG2E / heat
    put_rows(
        [-0.5 * inverse, ux * inverse, uy * inverse, uz * inverse]
        + [-0.5 * inverse * (ux * ux + uy * uy + uz * uz)],
        where,
        rhs,
        temp,
    )


def put_rows(values, where, rhs, temp):
    for place, value in enumerate(values):
        temp[place : place + 1, :] = value
    first, second, third = split3(temp[...])
    for place, part in enumerate((first, second, first, second, third, first)):
        rhs[place * GROUP : (place + 1) * GROUP, where] = part


def spread_rows(macro, step, where, points, moments, rhs, keep, temp):
    density, ux, uy, uz, heat = cell(macro, step, where)
    root = jnp.sqrt(heat)
    inv = 1.0 / root
    inv2 = inv * inv
    inv3 = inv2 * inv
    rate = 0.3 * density * root
    keep[:, where] = 1.0 - rate
    scale = density * inv3 * ((2.0 * math.pi) ** (-1.5) * REGION / points)
    m = [moments[pl.ds(k, 1), where] * scale for k in range(MODES)]
    u = (ux, uy, uz)
    u2 = ux * ux + uy * uy + uz * uz
    c1 = [m[1 + a] - u[a] * m[0] for a in range(3)]
    diag = [m[4 + a] - 2.0 * u[a] * m[1 + a] + u[a] * u[a] * m[0] for a in range(3)]
    pairs = ((0, 1), (0, 2), (1, 2))
    off = [
        m[7 + k] - u[a] * m[1 + b] - u[b] * m[1 + a] + u[a] * u[b] * m[0]
        for k, (a, b) in enumerate(pairs)
    ]
    raw = {(a, a): m[4 + a] for a in range(3)}
    for k, (a, b) in enumerate(pairs):
        raw[a, b] = raw[b, a] = m[7 + k]
    whole = m[4] + m[5] + m[6]
    flow = ux * m[1] + uy * m[2] + uz * m[3]
    common = whole - 2.0 * flow + u2 * m[0]
    c3 = [
        m[10 + a]
        - 2.0 * (ux * raw[a, 0] + uy * raw[a, 1] + uz * raw[a, 2])
        + u2 * m[1 + a]
        - u[a] * common
        for a in range(3)
    ]
    e0 = rate * m[0]
    e1 = [rate * inv * c1[a] for a in range(3)]
    e4 = rate * ((diag[0] + diag[1] + diag[2]) * inv2 - 3.0 * m[0]) * (1.0 / math.sqrt(6.0))
    half = -0.5 * rate
    eo = [half * inv2 * off[k] for k in range(3)]
    e8 = half * inv2 * (diag[0] - diag[1]) * 0.5
    e9 = half * inv2 * (diag[0] + diag[1] - 2.0 * diag[2]) * (1.0 / math.sqrt(12.0))
    root10 = 1.0 / math.sqrt(10.0)
    e3 = [
        (rate * (1.0 / 3.0)) * (inv3 * c3[a] - 5.0 * inv * c1[a]) * root10 for a in range(3)
    ]
    h0 = e0 - (3.0 / math.sqrt(6.0)) * e4
    lin = [inv * e1[a] - (5.0 * root10) * inv * e3[a] for a in range(3)]
    qa = e4 * (1.0 / math.sqrt(6.0))
    qb = e8 * 0.5
    qc = e9 * (1.0 / math.sqrt(12.0))
    qd = [inv2 * (qa + qb + qc), inv2 * (qa - qb + qc), inv2 * (qa - 2.0 * qc)]
    qo = [inv2 * eo[k] for k in range(3)]
    cubic = [(root10 * inv3) * e3[a] for a in range(3)]
    tau = cubic[0] * ux + cubic[1] * uy + cubic[2] * uz
    full = {(a, a): 2.0 * qd[a] for a in range(3)}
    for k, (a, b) in enumerate(pairs):
        full[a, b] = full[b, a] = qo[k]
    qu = [full[a, 0] * ux + full[a, 1] * uy + full[a, 2] * uz for a in range(3)]
    constant = (
        h0
        - (lin[0] * ux + lin[1] * uy + lin[2] * uz)
        - tau * u2
        + 0.5 * (qu[0] * ux + qu[1] * uy + qu[2] * uz)
    )
    linear = [lin[a] + u2 * cubic[a] + 2.0 * tau * u[a] - qu[a] for a in range(3)]
    square = [qd[a] - 2.0 * cubic[a] * u[a] - tau for a in range(3)]
    cross = [
        qo[k] - 2.0 * (cubic[a] * u[b] + cubic[b] * u[a]) for k, (a, b) in enumerate(pairs)
    ]
    put_rows([constant] + linear + square + cross + cubic, where, rhs, temp)


def shift_index(sign, cells, reach):
    lane = lax.broadcasted_iota(jnp.int32, sign.shape, 1)
    moved = lane + reach * sign.astype(jnp.int32)
    moved = jnp.where(moved < 0, moved + cells, moved)
    return jnp.where(moved >= cells, moved - cells, moved)


def take(values, index):
    return jnp.take_along_axis(values, index, axis=1, mode="promise_in_bounds")


def spread_columns(cols, coef, index):
    block, cells = index.shape[1:]
    for k in range(7):
        coef[k] = jnp.broadcast_to(cols[:, k : k + 1], (block, cells))
    sign_y = jnp.broadcast_to(cols[:, 7:8], (block, cells))
    index[0] = shift_index(sign_y, cells, 1)
    index[1] = shift_index(sign_y, cells, 2)


def move_y(values, coef, index, rows):
    return (
        coef[3, rows] * values
        + coef[4, rows] * take(values, index[0, rows])
        + coef[5, rows] * take(values, index[1, rows])
    )


def add_moments(weighted, tab, acc, where):
    high = weighted.astype(BF16)
    low = (weighted - high.astype(F32)).astype(BF16)
    acc[:, where] += mxu(tab[0 : 2 * GROUP, :], high)
    acc[0:GROUP, where] += mxu(tab[0:GROUP, :], low)


def main_kernel(first, step, points, chunk, *refs):
    if first:
        macro, field, lhs_e, tab, cols = refs[:5]
        refs = refs[5:]
    else:
        low, high, macro, field, lhs_r, lhs_e, tab, cols = refs[:8]
        refs = refs[8:]
    out, moments, coef, index, moved, weight, rhs_e, acc, temp = refs[:9]
    if not first:
        rhs_r, keep, spread, joint = refs[9:]
    wide = temp.shape[1]
    block, cells = index.shape[1:]
    rows_x = out.shape[0]
    total = rows_x * cells
    pairs = rows_x // 2
    here, last = pl.program_id(0), pl.num_programs(0) - 1

    @pl.when(here == 0)
    def _():
        temp[...] = jnp.zeros_like(temp)
        rhs_e[6 * GROUP :, :] = jnp.zeros((128 - 6 * GROUP, total), BF16)
        for edge in (0, 1, rows_x + 2, rows_x + 3):
            moved[edge] = jnp.zeros((block, cells), F32)
        acc[...] = jnp.zeros_like(acc)

        @pl.loop(0, total // wide)
        def _(k):
            where = pl.ds(pl.multiple_of(k * wide, wide), wide)
            exponent_rows(macro, step, where, rhs_e, temp)

        if not first:
            rhs_r[6 * GROUP :, :] = jnp.zeros((128 - 6 * GROUP, total), BF16)
            for p in range(pairs):
                half, q = (low, p) if p < pairs // 2 else (high, p - pairs // 2)
                joint[0:MODES, p * 2 * cells : (p + 1) * 2 * cells] = half[
                    q * MODES : (q + 1) * MODES, :
                ]
            temp[...] = jnp.zeros_like(temp)

            @pl.loop(0, total // wide)
            def _(k):
                where = pl.ds(pl.multiple_of(k * wide, wide), wide)
                spread_rows(macro, step + 1, where, points, joint, rhs_r, keep, temp)

    spread_columns(cols, coef, index)
    if first:
        flat = field.reshape(block * rows_x, cells)

    def along_y(p):
        where = pl.ds(pl.multiple_of(p * 2 * cells, 2 * cells), 2 * cells)
        exponent = mxu(lhs_e[...], rhs_e[:, where])
        for k in range(2):
            weight[2 * p + k] = jnp.exp2(exponent[:, k * cells : (k + 1) * cells])
        if not first:
            spread[...] = mxu(lhs_r[...], rhs_r[:, where])
        for start in range(0, block, chunk):
            rows = slice(start, start + chunk)
            for k in range(2):
                x = 2 * p + k
                if first:
                    values = flat[pl.ds(start * rows_x + x, chunk, stride=rows_x), :]
                else:
                    lane = pl.ds(pl.multiple_of(x * cells, cells), cells)
                    values = (
                        field[x, rows] * keep[:, lane]
                        + spread[rows, k * cells : (k + 1) * cells]
                    )
                moved[x + 2, rows] = move_y(values, coef, index, rows)

    def along_x(p):
        where = pl.ds(pl.multiple_of(p * 2 * cells, 2 * cells), 2 * cells)
        for start in range(0, block, chunk):
            rows = slice(start, start + chunk)
            line = [moved[2 * p + k, rows] for k in range(6)]
            positive = coef[6, rows] > 0.0
            for k in range(2):
                near = jnp.where(positive, line[k + 3], line[k + 1])
                far = jnp.where(positive, line[k + 4], line[k])
                value = (
                    coef[0, rows] * line[k + 2] + coef[1, rows] * near + coef[2, rows] * far
                )
                out[2 * p + k, rows] = value
                weight[2 * p + k, rows] = weight[2 * p + k, rows] * value
        weighted = jnp.concatenate([weight[2 * p], weight[2 * p + 1]], axis=1)
        add_moments(weighted, tab, acc, where)

    along_y(0)

    @pl.loop(0, pairs - 1)
    def _(p):
        along_y(p + 1)
        along_x(p)

    along_x(pairs - 1)

    @pl.when(here == last)
    def _():
        for p in range(pairs):
            where = slice(p * 2 * cells, (p + 1) * 2 * cells)
            sums = acc[0:GROUP, where] + acc[GROUP : 2 * GROUP, where]
            side, q = divmod(p, pairs // 2)
            moments[side, q * MODES : (q + 1) * MODES, :] = sums[0:MODES]


def whole(shape):
    return pl.BlockSpec(shape, lambda i: (0,) * len(shape))


def main_step(step, points, block, field, macro, tables, summed):
    lhs_r, lhs_e, tab, cols = tables
    first = summed is None
    if first:
        count, rows_x, cells = field.shape
        field_spec = pl.BlockSpec((block, rows_x, cells), lambda i: (i, 0, 0))
    else:
        rows_x, count, cells = field.shape
        field_spec = pl.BlockSpec((rows_x, block, cells), lambda i: (0, i, 0))
    total = rows_x * cells
    halves = (rows_x // 4) * MODES
    table_specs = [
        pl.BlockSpec((block, 128), lambda i: (i, 0)),
        pl.BlockSpec((3 * GROUP, block), lambda i: (0, i)),
        pl.BlockSpec((block, 128), lambda i: (i, 0)),
    ]
    if first:
        args = (macro, field, lhs_e, tab, cols)
        specs = [whole(macro.shape), field_spec] + table_specs
    else:
        args = (*summed, macro, field, lhs_r, lhs_e, tab, cols)
        specs = (
            [whole((halves, 2 * cells))] * 2
            + [whole(macro.shape), field_spec, table_specs[0]]
            + table_specs
        )
    scratch = [
        pltpu.VMEM((7, block, cells), F32),
        pltpu.VMEM((2, block, cells), jnp.int32),
        pltpu.VMEM((rows_x + 4, block, cells), F32),
        pltpu.VMEM((rows_x, block, cells), F32),
        pltpu.VMEM((128, total), BF16),
        pltpu.VMEM((2 * GROUP, total), F32),
        pltpu.VMEM((GROUP, min(512, total)), F32),
    ]
    if not first:
        scratch += [
            pltpu.VMEM((128, total), BF16),
            pltpu.VMEM((1, total), F32),
            pltpu.VMEM((block, 2 * cells), F32),
            pltpu.VMEM((GROUP, total), F32),
        ]
    return pl.pallas_call(
        functools.partial(main_kernel, first, step, points, min(32, block)),
        grid=(count // block,),
        in_specs=specs,
        out_specs=[
            pl.BlockSpec((rows_x, block, cells), lambda i: (0, i, 0)),
            whole((2, halves, 2 * cells)),
        ],
        out_shape=[
            jax.ShapeDtypeStruct((rows_x, count, cells), F32),
            jax.ShapeDtypeStruct((2, halves, 2 * cells), F32),
        ],
        scratch_shapes=scratch,
        compiler_params=pltpu.CompilerParams(vmem_limit_bytes=VMEM_LIMIT),
        cost_estimate=pl.CostEstimate(
            flops=20 * count * total, bytes_accessed=8 * count * total, transcendentals=0
        ),
        name="main",
    )(*args)


def edge_kernel(first, step, points, send, *refs):
    if first:
        macro, near_macro, before, after, lhs_e, tab, cols, sums, line = refs[:9]
        refs = refs[9:]
    else:
        near_sums, macro, near_macro, before, after = refs[:5]
        lhs_r, lhs_e, tab, cols, sums, line = refs[5:11]
        refs = refs[11:]
    line_out, sums_out = refs[:2]
    refs = refs[2:]
    if send:
        to_before, to_after = refs[:2]
        refs = refs[2:]
    coef, index, rhs_e, acc, temp = refs[:5]
    if not first:
        rhs_r, keep = refs[5:]
    block, cells = index.shape[1:]
    side, here = pl.program_id(0), pl.program_id(1)
    width = 2 * cells
    rows_half = sums.shape[1]

    @pl.when((side == 0) & (here == 0))
    def _():
        sums_out[...] = sums[...]

    @pl.when(here == 0)
    def _():
        temp[...] = jnp.zeros_like(temp)
        rhs_e[...] = jnp.zeros_like(rhs_e)
        acc[...] = jnp.zeros_like(acc)
        total = macro.shape[2]
        own = pl.ds(pl.multiple_of(side * (total - width), width), width)
        _, ux, uy, uz, heat = cell(macro, step, own)
        inverse = LOG2E / heat
        put_rows(
            [-0.5 * inverse, ux * inverse, uy * inverse, uz * inverse]
            + [-0.5 * inverse * (ux * ux + uy * uy + uz * uz)],
            slice(0, width),
            rhs_e,
            temp,
        )
        if not first:
            temp[...] = jnp.zeros_like(temp)
            rhs_r[...] = jnp.zeros_like(rhs_r)
            spread_rows(
                near_macro.at[side],
                step + 1,
                slice(0, width),
                points,
                near_sums.at[side],
                rhs_r,
                keep,
                temp,
            )

    spread_columns(cols, coef, index)
    weight = jnp.exp2(mxu(lhs_e[...], rhs_e[...]))
    if not first:
        returned = mxu(lhs_r[...], rhs_r[...])

    def finish(halo, mine):
        rows = slice(0, block)
        moved = []
        for k in range(2):
            values = halo[k] if not first else (halo[:, k] if False else halo[k])
            if not first:
                lane = slice(k * cells, (k + 1) * cells)
                values = values * keep[:, lane] + returned[:, lane]
            moved.append(move_y(values, coef, index, rows))
        if mine == 0:
            takes = coef[6] < 0.0
            extra = [
                coef[1] * moved[1] + coef[2] * moved[0],
                coef[2] * moved[1],
            ]
        else:
            takes = coef[6] > 0.0
            extra = [
                coef[2] * moved[0],
                coef[1] * moved[0] + coef[2] * moved[1],
            ]
        extra = [jnp.where(takes, value, 0.0) for value in extra]
        for k in range(2):
            value = line[k] + extra[k]
            line_out[k] = value
            if send:
                (to_before if mine == 0 else to_after)[k] = value
        add_moments(jnp.concatenate(extra, axis=1) * weight, tab, acc, slice(0, width))

        @pl.when(here == pl.num_programs(1) - 1)
        def _():
            extra_sums = acc[0:GROUP] + acc[GROUP : 2 * GROUP]
            at = 0 if mine == 0 else rows_half - MODES
            sums_out[mine, at : at + MODES, :] += extra_sums[0:MODES]

    @pl.when(side == 0)
    def _():
        finish(before, 0)

    @pl.when(side == 1)
    def _():
        finish(after, 1)


def edge_step(step, points, block, send, halo, line, sums, macro, near, tables, near_sums):
    lhs_r, lhs_e, tab, cols = tables
    near_macro = near
    first = near_sums is None
    rows_x, count, cells = line.shape
    blocks = count // block
    width = 2 * cells

    def full(shape):
        return pl.BlockSpec(shape, lambda s, i: (0,) * len(shape))

    by_rows = pl.BlockSpec((block, 128), lambda s, i: (i, 0))
    halo_before = pl.BlockSpec(
        (2, block, cells), lambda s, i: (0, jnp.where(s == 0, i, blocks - 1), 0)
    )
    halo_after = pl.BlockSpec((2, block, cells), lambda s, i: (0, jnp.where(s == 0, 0, i), 0))
    edge = pl.BlockSpec((2, block, cells), lambda s, i: (s * (rows_x // 2 - 1), i, 0))
    args = [macro, near_macro, *halo]
    specs = [full(macro.shape), full(near_macro.shape), halo_before, halo_after]
    if not first:
        args = [near_sums] + args + [lhs_r]
        specs = [full(near_sums.shape)] + specs + [by_rows]
    args += [lhs_e, tab, cols, sums, line]
    specs += [
        by_rows,
        pl.BlockSpec((3 * GROUP, block), lambda s, i: (0, i)),
        by_rows,
        full(sums.shape),
        edge,
    ]
    out_specs = [edge, full(sums.shape)]
    out_shape = [
        jax.ShapeDtypeStruct(line.shape, F32),
        jax.ShapeDtypeStruct(sums.shape, F32),
    ]
    if send:
        out_specs += [halo_before, halo_after]
        out_shape += [jax.ShapeDtypeStruct((2, count, cells), F32)] * 2
    scratch = [
        pltpu.VMEM((7, block, cells), F32),
        pltpu.VMEM((2, block, cells), jnp.int32),
        pltpu.VMEM((128, width), BF16),
        pltpu.VMEM((2 * GROUP, width), F32),
        pltpu.VMEM((GROUP, width), F32),
    ]
    if not first:
        scratch += [pltpu.VMEM((128, width), BF16), pltpu.VMEM((1, width), F32)]
    return pl.pallas_call(
        functools.partial(edge_kernel, first, step, points, send),
        grid=(2, blocks),
        in_specs=specs,
        out_specs=out_specs,
        out_shape=out_shape,
        scratch_shapes=scratch,
        input_output_aliases={len(args) - 1: 0},
        compiler_params=pltpu.CompilerParams(vmem_limit_bytes=VMEM_LIMIT),
        name="edge",
    )(*args)


def last_kernel(points, low, high, macro, field, lhs_r, out, rhs_r, keep, joint, temp):
    rows_x, block, cells = field.shape
    total = rows_x * cells
    pairs = rows_x // 2
    wide = temp.shape[1]

    @pl.when(pl.program_id(0) == 0)
    def _():
        temp[...] = jnp.zeros_like(temp)
        rhs_r[6 * GROUP :, :] = jnp.zeros((128 - 6 * GROUP, total), BF16)
        for p in range(pairs):
            half, q = (low, p) if p < pairs // 2 else (high, p - pairs // 2)
            joint[0:MODES, p * 2 * cells : (p + 1) * 2 * cells] = half[
                q * MODES : (q + 1) * MODES, :
            ]

        @pl.loop(0, total // wide)
        def _(k):
            where = pl.ds(pl.multiple_of(k * wide, wide), wide)
            spread_rows(macro, 0, where, points, joint, rhs_r, keep, temp)

    flat = out.reshape(block * rows_x, cells)

    @pl.loop(0, pairs)
    def _(p):
        where = pl.ds(pl.multiple_of(p * 2 * cells, 2 * cells), 2 * cells)
        returned = mxu(lhs_r[...], rhs_r[:, where])
        for k in range(2):
            x = 2 * p + k
            lane = pl.ds(pl.multiple_of(x * cells, cells), cells)
            flat[pl.ds(x, block, stride=rows_x), :] = (
                field[x] * keep[:, lane] + returned[:, k * cells : (k + 1) * cells]
            )


def last_step(points, block, field, macro, tables, summed):
    rows_x, count, cells = field.shape
    total = rows_x * cells
    halves = (rows_x // 4) * MODES
    return pl.pallas_call(
        functools.partial(last_kernel, points),
        grid=(count // block,),
        in_specs=[whole((halves, 2 * cells))] * 2
        + [
            whole(macro.shape),
            pl.BlockSpec((rows_x, block, cells), lambda i: (0, i, 0)),
            pl.BlockSpec((block, 128), lambda i: (i, 0)),
        ],
        out_specs=pl.BlockSpec((block, rows_x, cells), lambda i: (i, 0, 0)),
        out_shape=jax.ShapeDtypeStruct((count, rows_x, cells), F32),
        scratch_shapes=[
            pltpu.VMEM((128, total), BF16),
            pltpu.VMEM((1, total), F32),
            pltpu.VMEM((GROUP, total), F32),
            pltpu.VMEM((GROUP, min(512, total)), F32),
        ],
        compiler_params=pltpu.CompilerParams(vmem_limit_bytes=VMEM_LIMIT),
        name="last",
    )(*summed, macro, field, tables[0])


def sum_over_vel(halves):
    members = lax.axis_size("vel")
    me = lax.axis_index("vel")

    def partner(bit):
        return [(i, i ^ bit) for i in range(members)]

    own = lax.rem(me, 2)
    mine = lax.dynamic_index_in_dim(halves, own, 0, keepdims=False)
    other = lax.dynamic_index_in_dim(halves, 1 - own, 0, keepdims=False)
    mine = mine + lax.ppermute(other, "vel", partner(1))
    bit = 2
    while bit < members:
        mine = mine + lax.ppermute(mine, "vel", partner(bit))
        bit *= 2
    other = lax.ppermute(mine, "vel", partner(1))
    even = own == 0
    return jnp.where(even, mine, other), jnp.where(even, other, mine)


def from_sides(to_before, to_after):
    peers = lax.axis_size("space")
    up = [(i, (i + 1) % peers) for i in range(peers)]
    down = [(j, i) for i, j in up]
    return lax.ppermute(to_after, "space", up), lax.ppermute(to_before, "space", down)


def shards(cotangent, speed, direction, macroscopic_record):
    count, rows_x, cells = cotangent.shape
    points = count * lax.axis_size("vel")
    steps = macroscopic_record.shape[0]
    block = min(256, count)
    pairs = rows_x // 2
    width = 2 * cells

    halo = from_sides(
        jnp.transpose(cotangent[:, :2], (1, 0, 2)),
        jnp.transpose(cotangent[:, rows_x - 2 :], (1, 0, 2)),
    )
    macro = macroscopic_record.reshape(steps, 5, rows_x * cells)
    near = jnp.stack(from_sides(macro[:, :, :width], macro[:, :, -width:]))
    tables = make_tables(speed, direction)
    field, summed, near_sums = cotangent, None, None
    for step in range(steps - 1, -1, -1):
        line, sums = main_step(step, points, block, field, macro, tables, summed)
        send = step > 0
        results = edge_step(
            step, points, block, send, halo, line, sums, macro, near, tables, near_sums
        )
        field, sums = results[:2]
        if send:
            halo = from_sides(*results[2:])
        summed = sum_over_vel(sums)
        if send:
            near_sums = jnp.stack(from_sides(summed[0][:MODES], summed[1][-MODES:]))
    return last_step(points, block, field, macro, tables, summed)


def solution(mesh):
    in_specs = (
        P("vel", "space", None),
        P(None, "vel"),
        P(None, "vel"),
        P(None, None, "space", None),
    )
    out_specs = P("vel", "space", None)
    return jax.shard_map(shards, mesh=mesh, in_specs=in_specs, out_specs=out_specs, check_vma=False)
```

```python
import functools
import math

import jax
import jax.numpy as jnp
from jax import lax
from jax.experimental import pallas as pl
from jax.experimental.pallas import tpu as pltpu
from jax.sharding import PartitionSpec as P


F32, BF16 = jnp.float32, jnp.bfloat16
COURANT = 0.1
REGION = 216.0
BLOCK = 256
MODES = 13
GROUP = 16
LOG2E = math.log2(math.e)
VMEM_LIMIT = 60 * 1024 * 1024


def split3(x):
    high = x.astype(BF16)
    rest = x - high.astype(F32)
    middle = rest.astype(BF16)
    low = (rest - middle.astype(F32)).astype(BF16)
    return high, middle, low


def mxu(a, b):
    return jnp.dot(a, b, preferred_element_type=F32)


def tables_kernel(speed_ref, direction_ref, lhs_r, lhs_e, tab, cols, rows):
    count = speed_ref.shape[1]
    sign = (2 * direction_ref[...] - 1).astype(F32)
    speed = speed_ref[...]
    velocity = sign * speed
    vx, vy, vz = (velocity[k : k + 1] for k in range(3))
    square = vx * vx + vy * vy + vz * vz
    one = jnp.ones_like(vx)

    def put(values):
        rows[0:GROUP, :] = jnp.zeros((GROUP, count), F32)
        for place, value in enumerate(values):
            rows[place : place + 1, :] = value
        return split3(rows[0:GROUP, :])

    def left(parts):
        first, second, third = (part.astype(F32) for part in parts)
        for place, part in enumerate((first, first, second, second, first, third)):
            rows[place * GROUP : (place + 1) * GROUP, :] = part
        rows[6 * GROUP :, :] = jnp.zeros((rows.shape[0] - 6 * GROUP, count), F32)
        return rows[...].T.astype(BF16)

    parts = put(
        [one, vx, vy, vz, vx * vx, vy * vy, vz * vz, vx * vy, vx * vz, vy * vz]
        + [vx * square, vy * square, vz * square]
    )
    for place, part in enumerate(parts):
        tab[place * GROUP : (place + 1) * GROUP, :] = part
    lhs_r[...] = left(parts)
    lhs_e[...] = left(put([square, vx, vy, vz, one]))
    rows[...] = jnp.zeros_like(rows)
    lam = COURANT * speed
    rows[0:1, :] = 1.0 - 1.5 * lam[0:1]
    rows[1:2, :] = 2.0 * lam[0:1]
    rows[2:3, :] = -0.5 * lam[0:1]
    rows[3:4, :] = -0.5 * lam[1:2]
    rows[4:6, :] = sign[0:2]
    cols[...] = rows[...].T


def make_tables(speed, direction):
    count = speed.shape[1]
    return pl.pallas_call(
        tables_kernel,
        out_shape=(
            jax.ShapeDtypeStruct((count, 128), BF16),
            jax.ShapeDtypeStruct((count, 128), BF16),
            jax.ShapeDtypeStruct((3 * GROUP, count), BF16),
            jax.ShapeDtypeStruct((count, 128), F32),
        ),
        scratch_shapes=[pltpu.VMEM((128, count), F32)],
        name="tables",
    )(speed, direction)


def cell(macro, step, where):
    return [macro[step, pl.ds(k, 1), where] for k in range(5)]


def exponent_rows(macro, step, where, rhs, temp, into=None):
    _, ux, uy, uz, heat = cell(macro, step, where)
    inverse = LOG2E / heat
    put_rows(
        [-0.5 * inverse, ux * inverse, uy * inverse, uz * inverse]
        + [-0.5 * inverse * (ux * ux + uy * uy + uz * uz)],
        where if into is None else into,
        rhs,
        temp,
    )


def put_rows(values, where, rhs, temp):
    count = values[0].shape[1]
    for place, value in enumerate(values):
        temp[place : place + 1, 0:count] = value
    first, second, third = split3(temp[:, 0:count])
    for place, part in enumerate((first, second, first, second, third, first)):
        rhs[place * GROUP : (place + 1) * GROUP, where] = part


def spread_rows(macro, step, where, points, moments, rhs, keep, temp):
    density, ux, uy, uz, heat = cell(macro, step, where)
    root = jnp.sqrt(heat)
    inv = 1.0 / root
    inv2 = inv * inv
    inv3 = inv2 * inv
    rate = 0.3 * density * root
    keep[:, where] = 1.0 - rate
    scale = density * inv3 * ((2.0 * math.pi) ** (-1.5) * REGION / points)
    m = [moments[pl.ds(k, 1), where] * scale for k in range(MODES)]
    u = (ux, uy, uz)
    u2 = ux * ux + uy * uy + uz * uz
    c1 = [m[1 + a] - u[a] * m[0] for a in range(3)]
    diag = [m[4 + a] - 2.0 * u[a] * m[1 + a] + u[a] * u[a] * m[0] for a in range(3)]
    pairs = ((0, 1), (0, 2), (1, 2))
    off = [
        m[7 + k] - u[a] * m[1 + b] - u[b] * m[1 + a] + u[a] * u[b] * m[0]
        for k, (a, b) in enumerate(pairs)
    ]
    raw = {(a, a): m[4 + a] for a in range(3)}
    for k, (a, b) in enumerate(pairs):
        raw[a, b] = raw[b, a] = m[7 + k]
    whole = m[4] + m[5] + m[6]
    flow = ux * m[1] + uy * m[2] + uz * m[3]
    common = whole - 2.0 * flow + u2 * m[0]
    c3 = [
        m[10 + a]
        - 2.0 * (ux * raw[a, 0] + uy * raw[a, 1] + uz * raw[a, 2])
        + u2 * m[1 + a]
        - u[a] * common
        for a in range(3)
    ]
    e0 = rate * m[0]
    e1 = [rate * inv * c1[a] for a in range(3)]
    e4 = rate * ((diag[0] + diag[1] + diag[2]) * inv2 - 3.0 * m[0]) * (1.0 / math.sqrt(6.0))
    half = -0.5 * rate
    eo = [half * inv2 * off[k] for k in range(3)]
    e8 = half * inv2 * (diag[0] - diag[1]) * 0.5
    e9 = half * inv2 * (diag[0] + diag[1] - 2.0 * diag[2]) * (1.0 / math.sqrt(12.0))
    root10 = 1.0 / math.sqrt(10.0)
    e3 = [
        (rate * (1.0 / 3.0)) * (inv3 * c3[a] - 5.0 * inv * c1[a]) * root10 for a in range(3)
    ]
    h0 = e0 - (3.0 / math.sqrt(6.0)) * e4
    lin = [inv * e1[a] - (5.0 * root10) * inv * e3[a] for a in range(3)]
    qa = e4 * (1.0 / math.sqrt(6.0))
    qb = e8 * 0.5
    qc = e9 * (1.0 / math.sqrt(12.0))
    qd = [inv2 * (qa + qb + qc), inv2 * (qa - qb + qc), inv2 * (qa - 2.0 * qc)]
    qo = [inv2 * eo[k] for k in range(3)]
    cubic = [(root10 * inv3) * e3[a] for a in range(3)]
    tau = cubic[0] * ux + cubic[1] * uy + cubic[2] * uz
    full = {(a, a): 2.0 * qd[a] for a in range(3)}
    for k, (a, b) in enumerate(pairs):
        full[a, b] = full[b, a] = qo[k]
    qu = [full[a, 0] * ux + full[a, 1] * uy + full[a, 2] * uz for a in range(3)]
    constant = (
        h0
        - (lin[0] * ux + lin[1] * uy + lin[2] * uz)
        - tau * u2
        + 0.5 * (qu[0] * ux + qu[1] * uy + qu[2] * uz)
    )
    linear = [lin[a] + u2 * cubic[a] + 2.0 * tau * u[a] - qu[a] for a in range(3)]
    square = [qd[a] - 2.0 * cubic[a] * u[a] - tau for a in range(3)]
    cross = [
        qo[k] - 2.0 * (cubic[a] * u[b] + cubic[b] * u[a]) for k, (a, b) in enumerate(pairs)
    ]
    put_rows([constant] + linear + square + cross + cubic, where, rhs, temp)


def stencil(cells):
    source = lax.broadcasted_iota(jnp.int32, (2 * cells, 2 * cells), 0)
    target = lax.broadcasted_iota(jnp.int32, (2 * cells, 2 * cells), 1)
    source = jnp.where(source >= cells, source - cells, source)
    up = target < cells
    target = jnp.where(up, target, target - cells)
    ahead = jnp.where(up, source - target, target - source)
    ahead = jnp.where(ahead < 0, ahead + cells, ahead)
    values = jnp.where(ahead == 0, 3.0, 0.0) + jnp.where(ahead == 1, -4.0, 0.0)
    return (values + jnp.where(ahead == 2, 1.0, 0.0)).astype(BF16)


def spread_columns(cols, coef):
    block, cells = coef.shape[1:]
    for k in range(6):
        coef[k] = jnp.broadcast_to(cols[:, k : k + 1], (block, cells))


def split2(values):
    high = values.astype(BF16)
    return high, (values - high.astype(F32)).astype(BF16)


def move_y(values, coef, matrix):
    cells = values.shape[1]
    both = mxu(jnp.concatenate(split2(values), axis=1), matrix[...])
    change = jnp.where(coef[5] > 0.0, both[:, :cells], both[:, cells:])
    return values + coef[3] * change


def add_moments(weighted, tab, acc, where):
    high, low = split2(weighted)
    sums = mxu(tab[0 : 2 * GROUP, :], high)
    acc[:, where] = acc[:, where] + (
        sums[0:GROUP] + sums[GROUP : 2 * GROUP] + mxu(tab[0:GROUP, :], low)
    )


def main_kernel(first, step, points, *refs):
    if first:
        macro, field, lhs_e, tab, cols = refs[:5]
        refs = refs[5:]
    else:
        low, high, macro, field, edge_low, edge_high, lhs_r, lhs_e, tab, cols = refs[:10]
        refs = refs[10:]
    out, moments, coef, moved, matrix, rhs_e, acc, temp, parts, heavy = refs[:10]
    if first:
        (turned,) = refs[10:]
    else:
        rhs_r, keep, joint = refs[10:]
    wide = temp.shape[1]
    block, cells = coef.shape[1:]
    chunk = min(32, block)
    rows_x = out.shape[0]
    total = rows_x * cells
    pairs = rows_x // 2
    here, last = pl.program_id(0), pl.num_programs(0) - 1

    @pl.when(here == 0)
    def _():
        temp[...] = jnp.zeros_like(temp)
        matrix[...] = stencil(cells)
        rhs_e[6 * GROUP :, :] = jnp.zeros((128 - 6 * GROUP, total), BF16)
        for edge in (0, 1, rows_x + 2, rows_x + 3):
            moved[edge] = jnp.zeros((block, cells), F32)
        acc[...] = jnp.zeros_like(acc)

        @pl.loop(0, total // wide)
        def _(k):
            where = pl.ds(pl.multiple_of(k * wide, wide), wide)
            exponent_rows(macro, step, where, rhs_e, temp)

        if not first:
            rhs_r[6 * GROUP :, :] = jnp.zeros((128 - 6 * GROUP, total), BF16)
            for p in range(pairs):
                half, q = (low, p) if p < pairs // 2 else (high, p - pairs // 2)
                joint[0:MODES, p * 2 * cells : (p + 1) * 2 * cells] = half[
                    q * MODES : (q + 1) * MODES, :
                ]
            temp[...] = jnp.zeros_like(temp)

            @pl.loop(0, total // wide)
            def _(k):
                where = pl.ds(pl.multiple_of(k * wide, wide), wide)
                spread_rows(macro, step + 1, where, points, joint, rhs_r, keep, temp)

    spread_columns(cols, coef)
    if first:
        for v in range(0, block, 8):
            for x in range(0, rows_x, 8):
                turned[x : x + 8, v : v + 8] = jnp.swapaxes(field[v : v + 8, x : x + 8], 0, 1)
        field = turned

    def layer(x, rows):
        if not first and x < 2:
            return edge_low[x, rows]
        if not first and x >= rows_x - 2:
            return edge_high[x - rows_x + 2, rows]
        return field[x, rows]

    def along_y(p):
        if not first:
            returned = mxu(lhs_r[...], rhs_r[:, p * 2 * cells : (p + 1) * 2 * cells])
        for k in range(2):
            x = 2 * p + k
            for start in range(0, block, chunk):
                rows = slice(start, start + chunk)
                values = layer(x, rows)
                if not first:
                    values = (
                        values * keep[:, x * cells : (x + 1) * cells]
                        + returned[rows, k * cells : (k + 1) * cells]
                    )
                moved[x + 2, rows] = values
                high, low = split2(values)
                parts[x % 4, rows, 0:cells] = high
                parts[x % 4, rows, cells:] = low
            both = mxu(parts[x % 4], matrix[...])
            for start in range(0, block, chunk):
                rows = slice(start, start + chunk)
                change = jnp.where(coef[5, rows] > 0.0, both[rows, :cells], both[rows, cells:])
                moved[x + 2, rows] = moved[x + 2, rows] + coef[3, rows] * change

    def along_x(p):
        where = slice(p * 2 * cells, (p + 1) * 2 * cells)
        exponent = mxu(lhs_e[...], rhs_e[:, where])
        for start in range(0, block, chunk):
            rows = slice(start, start + chunk)
            line = [moved[2 * p + k, rows] for k in range(6)]
            positive = coef[4, rows] > 0.0
            for k in range(2):
                near = jnp.where(positive, line[k + 3], line[k + 1])
                far = jnp.where(positive, line[k + 4], line[k])
                value = coef[0, rows] * line[k + 2] + coef[1, rows] * near + coef[2, rows] * far
                out[2 * p + k, rows] = value
                high, low = split2(jnp.exp2(exponent[rows, k * cells : (k + 1) * cells]) * value)
                heavy[p % 2, 0, rows, k * cells : (k + 1) * cells] = high
                heavy[p % 2, 1, rows, k * cells : (k + 1) * cells] = low
        sums = mxu(tab[0 : 2 * GROUP, :], heavy[p % 2, 0])
        acc[:, where] = acc[:, where] + (
            sums[0:GROUP] + sums[GROUP : 2 * GROUP] + mxu(tab[0:GROUP, :], heavy[p % 2, 1])
        )

    along_y(0)
    for p in range(pairs):
        if p + 1 < pairs:
            along_y(p + 1)
        along_x(p)

    @pl.when(here == last)
    def _():
        for p in range(pairs):
            where = slice(p * 2 * cells, (p + 1) * 2 * cells)
            side, q = divmod(p, pairs // 2)
            moments[side, q * MODES : (q + 1) * MODES, :] = acc[0:MODES, where]


def whole(shape):
    return pl.BlockSpec(shape, lambda i: (0,) * len(shape))


def main_step(step, points, block, field, macro, tables, summed, edges=None):
    lhs_r, lhs_e, tab, cols = tables
    first = summed is None
    if first:
        count, rows_x, cells = field.shape
        field_spec = pl.BlockSpec((block, rows_x, cells), lambda i: (i, 0, 0))
    else:
        rows_x, count, cells = field.shape
        field_spec = pl.BlockSpec((rows_x, block, cells), lambda i: (0, i, 0))
    total = rows_x * cells
    halves = (rows_x // 4) * MODES
    table_specs = [
        pl.BlockSpec((block, 128), lambda i: (i, 0)),
        pl.BlockSpec((3 * GROUP, block), lambda i: (0, i)),
        pl.BlockSpec((block, 128), lambda i: (i, 0)),
    ]
    if first:
        args = (macro, field, lhs_e, tab, cols)
        specs = [whole(macro.shape), field_spec] + table_specs
    else:
        args = (*summed, macro, field, *edges, lhs_r, lhs_e, tab, cols)
        edge_spec = pl.BlockSpec((2, block, cells), lambda i: (0, i, 0))
        specs = (
            [whole((halves, 2 * cells))] * 2
            + [whole(macro.shape), field_spec, edge_spec, edge_spec, table_specs[0]]
            + table_specs
        )
    scratch = [
        pltpu.VMEM((6, block, cells), F32),
        pltpu.VMEM((rows_x + 4, block, cells), F32),
        pltpu.VMEM((2 * cells, 2 * cells), BF16),
        pltpu.VMEM((128, total), BF16),
        pltpu.VMEM((GROUP, total), F32),
        pltpu.VMEM((GROUP, min(512, total)), F32),
        pltpu.VMEM((4, block, 2 * cells), BF16),
        pltpu.VMEM((2, 2, block, 2 * cells), BF16),
    ]
    if first:
        scratch += [pltpu.VMEM((rows_x, block, cells), F32)]
    else:
        scratch += [
            pltpu.VMEM((128, total), BF16),
            pltpu.VMEM((1, total), F32),
            pltpu.VMEM((GROUP, total), F32),
        ]
    return pl.pallas_call(
        functools.partial(main_kernel, first, step, points),
        grid=(count // block,),
        in_specs=specs,
        out_specs=[
            pl.BlockSpec((rows_x, block, cells), lambda i: (0, i, 0)),
            whole((2, halves, 2 * cells)),
        ],
        out_shape=[
            jax.ShapeDtypeStruct((rows_x, count, cells), F32),
            jax.ShapeDtypeStruct((2, halves, 2 * cells), F32),
        ],
        scratch_shapes=scratch,
        compiler_params=pltpu.CompilerParams(vmem_limit_bytes=VMEM_LIMIT),
        cost_estimate=pl.CostEstimate(
            flops=20 * count * total, bytes_accessed=8 * count * total, transcendentals=0
        ),
        name="main",
    )(*args)


def edge_kernel(first, step, points, *refs):
    if first:
        macro, before, after, lhs_e, tab, cols, sums, line_low, line_high = refs[:9]
        refs = refs[9:]
    else:
        near_sums, near_macro, macro, before, after = refs[:5]
        lhs_r, lhs_e, tab, cols, sums, line_low, line_high = refs[5:12]
        refs = refs[12:]
    low_out, high_out, sums_low, sums_high, coef, matrix, rhs_e, acc, temp = refs[:9]
    if not first:
        rhs_r, keep = refs[9:]
    block, cells = coef.shape[1:]
    width = 2 * cells
    rows_half = sums.shape[1]
    here = pl.program_id(0)

    @pl.when(here == 0)
    def _():
        temp[...] = jnp.zeros_like(temp)
        matrix[...] = stencil(cells)
        acc[...] = jnp.zeros_like(acc)
        rhs_e[...] = jnp.zeros_like(rhs_e)
        total = macro.shape[2]
        for side in range(2):
            own = slice(side * (total - width), side * (total - width) + width)
            into = slice(side * width, side * width + width)
            exponent_rows(macro, step, own, rhs_e, temp, into)
        if not first:
            temp[...] = jnp.zeros_like(temp)
            rhs_r[...] = jnp.zeros_like(rhs_r)
            spread_rows(
                near_macro, step + 1, slice(0, 2 * width), points, near_sums, rhs_r, keep, temp
            )

    spread_columns(cols, coef)
    sign = coef[4]
    for side, halo in enumerate((before, after)):
        lanes = slice(side * width, side * width + width)
        weight = jnp.exp2(mxu(lhs_e[...], rhs_e[:, lanes]))
        if not first:
            returned = mxu(lhs_r[...], rhs_r[:, lanes])
        moved = []
        for k in range(2):
            values = halo[k]
            if not first:
                lane = slice(k * cells, (k + 1) * cells)
                values = values * keep[:, side * width + k * cells :][:, :cells]
                values = values + returned[:, lane]
            moved.append(move_y(values, coef, matrix))
        if side == 0:
            takes = sign < 0.0
            extra = [coef[1] * moved[1] + coef[2] * moved[0], coef[2] * moved[1]]
        else:
            takes = sign > 0.0
            extra = [coef[2] * moved[0], coef[1] * moved[0] + coef[2] * moved[1]]
        extra = [jnp.where(takes, value, 0.0) for value in extra]
        for k in range(2):
            if side == 0:
                low_out[k] = line_low[k] + extra[k]
            else:
                high_out[k] = line_high[k] + extra[k]
        add_moments(jnp.concatenate(extra, axis=1) * weight, tab, acc, lanes)

    @pl.when(here == pl.num_programs(0) - 1)
    def _():
        sums_low[...] = sums[0]
        sums_high[...] = sums[1]
        sums_low[0:MODES, :] = sums[0, 0:MODES] + acc[0:MODES, 0:width]
        sums_high[rows_half - MODES :, :] = sums[1, rows_half - MODES :] + acc[0:MODES, width:]


def edge_step(step, points, block, halo, line, sums, macro, near, tables, near_sums):
    lhs_r, lhs_e, tab, cols = tables
    first = near_sums is None
    rows_x, count, cells = line.shape
    width = 2 * cells
    by_rows = pl.BlockSpec((block, 128), lambda i: (i, 0))
    by_layers = pl.BlockSpec((2, block, cells), lambda i: (0, i, 0))
    by_columns = pl.BlockSpec((3 * GROUP, block), lambda i: (0, i))
    line_high = pl.BlockSpec((2, block, cells), lambda i: (rows_x // 2 - 1, i, 0))
    args, specs = [macro, *halo], [whole(macro.shape), by_layers, by_layers]
    if not first:
        args = [near_sums, near] + args + [lhs_r]
        specs = [whole(near_sums.shape), whole(near.shape)] + specs + [by_rows]
    args += [lhs_e, tab, cols, sums, line, line]
    specs += [by_rows, by_columns, by_rows, whole(sums.shape), by_layers, line_high]
    scratch = [
        pltpu.VMEM((6, block, cells), F32),
        pltpu.VMEM((width, width), BF16),
        pltpu.VMEM((128, 2 * width), BF16),
        pltpu.VMEM((GROUP, 2 * width), F32),
        pltpu.VMEM((GROUP, 2 * width), F32),
    ]
    if not first:
        scratch += [pltpu.VMEM((128, 2 * width), BF16), pltpu.VMEM((1, 2 * width), F32)]
    return pl.pallas_call(
        functools.partial(edge_kernel, first, step, points),
        grid=(count // block,),
        in_specs=specs,
        out_specs=[by_layers, by_layers] + [whole(sums.shape[1:])] * 2,
        out_shape=[jax.ShapeDtypeStruct((2, count, cells), F32)] * 2
        + [jax.ShapeDtypeStruct(sums.shape[1:], F32)] * 2,
        scratch_shapes=scratch,
        compiler_params=pltpu.CompilerParams(vmem_limit_bytes=VMEM_LIMIT),
        name="edge",
    )(*args)


def last_kernel(
    points, low, high, macro, field, edge_low, edge_high, lhs_r, out, rhs_r, keep, joint, temp, turned
):
    rows_x, block, cells = field.shape
    total = rows_x * cells
    pairs = rows_x // 2
    wide = temp.shape[1]

    @pl.when(pl.program_id(0) == 0)
    def _():
        temp[...] = jnp.zeros_like(temp)
        rhs_r[6 * GROUP :, :] = jnp.zeros((128 - 6 * GROUP, total), BF16)
        for p in range(pairs):
            half, q = (low, p) if p < pairs // 2 else (high, p - pairs // 2)
            joint[0:MODES, p * 2 * cells : (p + 1) * 2 * cells] = half[
                q * MODES : (q + 1) * MODES, :
            ]

        @pl.loop(0, total // wide)
        def _(k):
            where = pl.ds(pl.multiple_of(k * wide, wide), wide)
            spread_rows(macro, 0, where, points, joint, rhs_r, keep, temp)

    for x in range(0, rows_x, 8):
        for p in range(x // 2, x // 2 + 4):
            returned = mxu(lhs_r[...], rhs_r[:, p * 2 * cells : (p + 1) * 2 * cells])
            for k in range(2):
                lane = slice((2 * p + k) * cells, (2 * p + k + 1) * cells)
                if p == 0:
                    values = edge_low[k]
                elif p == pairs - 1:
                    values = edge_high[k]
                else:
                    values = field[2 * p + k]
                turned[2 * p + k - x] = (
                    values * keep[:, lane] + returned[:, k * cells : (k + 1) * cells]
                )
        for v in range(0, block, 8):
            out[v : v + 8, x : x + 8] = jnp.swapaxes(turned[:, v : v + 8], 0, 1)


def last_step(points, block, field, macro, tables, summed, edges):
    rows_x, count, cells = field.shape
    total = rows_x * cells
    halves = (rows_x // 4) * MODES
    return pl.pallas_call(
        functools.partial(last_kernel, points),
        grid=(count // block,),
        in_specs=[whole((halves, 2 * cells))] * 2
        + [
            whole(macro.shape),
            pl.BlockSpec((rows_x, block, cells), lambda i: (0, i, 0)),
            pl.BlockSpec((2, block, cells), lambda i: (0, i, 0)),
            pl.BlockSpec((2, block, cells), lambda i: (0, i, 0)),
            pl.BlockSpec((block, 128), lambda i: (i, 0)),
        ],
        out_specs=pl.BlockSpec((block, rows_x, cells), lambda i: (i, 0, 0)),
        out_shape=jax.ShapeDtypeStruct((count, rows_x, cells), F32),
        scratch_shapes=[
            pltpu.VMEM((128, total), BF16),
            pltpu.VMEM((1, total), F32),
            pltpu.VMEM((GROUP, total), F32),
            pltpu.VMEM((GROUP, min(512, total)), F32),
            pltpu.VMEM((8, block, cells), F32),
        ],
        compiler_params=pltpu.CompilerParams(vmem_limit_bytes=VMEM_LIMIT),
        name="last",
    )(*summed, macro, field, *edges, tables[0])


def sum_over_vel(low, high):
    members = lax.axis_size("vel")
    even = lax.rem(lax.axis_index("vel"), 2) == 0

    def partner(bit):
        return [(i, i ^ bit) for i in range(members)]

    mine = jnp.where(even, low, high)
    mine = mine + lax.ppermute(jnp.where(even, high, low), "vel", partner(1))
    bit = 2
    while bit < members:
        mine = mine + lax.ppermute(mine, "vel", partner(bit))
        bit *= 2
    other = lax.ppermute(mine, "vel", partner(1))
    return jnp.where(even, mine, other), jnp.where(even, other, mine)


def from_sides(to_before, to_after):
    peers = lax.axis_size("space")
    up = [(i, (i + 1) % peers) for i in range(peers)]
    down = [(j, i) for i, j in up]
    return lax.ppermute(to_after, "space", up), lax.ppermute(to_before, "space", down)


def shards(cotangent, speed, direction, macroscopic_record):
    count, rows_x, cells = cotangent.shape
    points = count * lax.axis_size("vel")
    steps = macroscopic_record.shape[0]
    block = min(BLOCK, count)
    width = 2 * cells

    def with_cells(where):
        record = macroscopic_record[:, :, where].reshape(steps * 5, 2, cells)
        record = jnp.pad(record, ((0, -steps * 5 % 8), (0, 0), (0, 0)))
        return jnp.transpose(jnp.concatenate([cotangent[:, where], record]), (1, 0, 2))

    halo = from_sides(with_cells(slice(0, 2)), with_cells(slice(rows_x - 2, rows_x)))
    near = jnp.concatenate(
        [
            jnp.transpose(part[:, count : count + steps * 5], (1, 0, 2)).reshape(steps, 5, width)
            for part in halo
        ],
        axis=2,
    )
    macro = macroscopic_record.reshape(steps, 5, rows_x * cells)
    tables = make_tables(speed, direction)
    field, summed, near_sums, edges = cotangent, None, None, None
    for step in range(steps - 1, -1, -1):
        field, sums = main_step(step, points, block, field, macro, tables, summed, edges)
        *edges, low, high = edge_step(
            step, points, min(256, count), halo, field, sums, macro, near, tables, near_sums
        )
        if step > 0:
            halo = from_sides(*edges)
        summed = sum_over_vel(low, high)
        if step > 0:
            near_sums = jnp.concatenate(
                from_sides(summed[0][:MODES], summed[1][-MODES:]), axis=1
            )
    return last_step(points, min(128, count), field, macro, tables, summed, edges)


def solution(mesh):
    in_specs = (
        P("vel", "space", None),
        P(None, "vel"),
        P(None, "vel"),
        P(None, None, "space", None),
    )
    out_specs = P("vel", "space", None)
    return jax.shard_map(shards, mesh=mesh, in_specs=in_specs, out_specs=out_specs, check_vma=False)
```

```python
import functools
import math

import jax
import jax.numpy as jnp
from jax import lax
from jax.experimental import pallas as pl
from jax.experimental.pallas import tpu as pltpu
from jax.sharding import PartitionSpec as P


F32, BF16 = jnp.float32, jnp.bfloat16
COURANT = 0.1
REGION = 216.0
BLOCK = 256
MODES = 13
GROUP = 16
LOG2E = math.log2(math.e)
VMEM_LIMIT = 60 * 1024 * 1024


def split3(x):
    high = x.astype(BF16)
    rest = x - high.astype(F32)
    middle = rest.astype(BF16)
    low = (rest - middle.astype(F32)).astype(BF16)
    return high, middle, low


def mxu(a, b):
    return jnp.dot(a, b, preferred_element_type=F32)


def tables_kernel(speed_ref, direction_ref, lhs_r, lhs_e, tab, cols, rows):
    count = speed_ref.shape[1]
    sign = (2 * direction_ref[...] - 1).astype(F32)
    speed = speed_ref[...]
    velocity = sign * speed
    vx, vy, vz = (velocity[k : k + 1] for k in range(3))
    square = vx * vx + vy * vy + vz * vz
    one = jnp.ones_like(vx)

    def put(values):
        rows[0:GROUP, :] = jnp.zeros((GROUP, count), F32)
        for place, value in enumerate(values):
            rows[place : place + 1, :] = value
        return split3(rows[0:GROUP, :])

    def left(parts):
        first, second, third = (part.astype(F32) for part in parts)
        for place, part in enumerate((first, first, second, second, first, third)):
            rows[place * GROUP : (place + 1) * GROUP, :] = part
        rows[6 * GROUP :, :] = jnp.zeros((rows.shape[0] - 6 * GROUP, count), F32)
        return rows[...].T.astype(BF16)

    parts = put(
        [one, vx, vy, vz, vx * vx, vy * vy, vz * vz, vx * vy, vx * vz, vy * vz]
        + [vx * square, vy * square, vz * square]
    )
    for place, part in enumerate(parts):
        tab[place * GROUP : (place + 1) * GROUP, :] = part
    lhs_r[...] = left(parts)
    lhs_e[...] = left(put([square, vx, vy, vz, one]))
    rows[...] = jnp.zeros_like(rows)
    lam = COURANT * speed
    rows[0:1, :] = 1.0 - 1.5 * lam[0:1]
    rows[1:2, :] = 2.0 * lam[0:1]
    rows[2:3, :] = -0.5 * lam[0:1]
    rows[3:4, :] = -0.5 * lam[1:2]
    rows[4:6, :] = sign[0:2]
    cols[...] = rows[...].T


def make_tables(speed, direction):
    count = speed.shape[1]
    return pl.pallas_call(
        tables_kernel,
        out_shape=(
            jax.ShapeDtypeStruct((count, 128), BF16),
            jax.ShapeDtypeStruct((count, 128), BF16),
            jax.ShapeDtypeStruct((3 * GROUP, count), BF16),
            jax.ShapeDtypeStruct((count, 128), F32),
        ),
        scratch_shapes=[pltpu.VMEM((128, count), F32)],
        name="tables",
    )(speed, direction)


def cell(macro, step, where):
    return [macro[step, pl.ds(k, 1), where] for k in range(5)]


def exponent_rows(macro, step, where, rhs, temp, into=None):
    _, ux, uy, uz, heat = cell(macro, step, where)
    inverse = LOG2E / heat
    put_rows(
        [-0.5 * inverse, ux * inverse, uy * inverse, uz * inverse]
        + [-0.5 * inverse * (ux * ux + uy * uy + uz * uz)],
        where if into is None else into,
        rhs,
        temp,
    )


def put_rows(values, where, rhs, temp):
    count = values[0].shape[1]
    for place, value in enumerate(values):
        temp[place : place + 1, 0:count] = value
    first, second, third = split3(temp[:, 0:count])
    for place, part in enumerate((first, second, first, second, third, first)):
        rhs[place * GROUP : (place + 1) * GROUP, where] = part


def spread_rows(macro, step, where, points, moments, rhs, keep, temp):
    density, ux, uy, uz, heat = cell(macro, step, where)
    root = jnp.sqrt(heat)
    inv = 1.0 / root
    inv2 = inv * inv
    inv3 = inv2 * inv
    rate = 0.3 * density * root
    keep[:, where] = 1.0 - rate
    scale = density * inv3 * ((2.0 * math.pi) ** (-1.5) * REGION / points)
    m = [moments[pl.ds(k, 1), where] * scale for k in range(MODES)]
    u = (ux, uy, uz)
    u2 = ux * ux + uy * uy + uz * uz
    c1 = [m[1 + a] - u[a] * m[0] for a in range(3)]
    diag = [m[4 + a] - 2.0 * u[a] * m[1 + a] + u[a] * u[a] * m[0] for a in range(3)]
    pairs = ((0, 1), (0, 2), (1, 2))
    off = [
        m[7 + k] - u[a] * m[1 + b] - u[b] * m[1 + a] + u[a] * u[b] * m[0]
        for k, (a, b) in enumerate(pairs)
    ]
    raw = {(a, a): m[4 + a] for a in range(3)}
    for k, (a, b) in enumerate(pairs):
        raw[a, b] = raw[b, a] = m[7 + k]
    whole = m[4] + m[5] + m[6]
    flow = ux * m[1] + uy * m[2] + uz * m[3]
    common = whole - 2.0 * flow + u2 * m[0]
    c3 = [
        m[10 + a]
        - 2.0 * (ux * raw[a, 0] + uy * raw[a, 1] + uz * raw[a, 2])
        + u2 * m[1 + a]
        - u[a] * common
        for a in range(3)
    ]
    e0 = rate * m[0]
    e1 = [rate * inv * c1[a] for a in range(3)]
    e4 = rate * ((diag[0] + diag[1] + diag[2]) * inv2 - 3.0 * m[0]) * (1.0 / math.sqrt(6.0))
    half = -0.5 * rate
    eo = [half * inv2 * off[k] for k in range(3)]
    e8 = half * inv2 * (diag[0] - diag[1]) * 0.5
    e9 = half * inv2 * (diag[0] + diag[1] - 2.0 * diag[2]) * (1.0 / math.sqrt(12.0))
    root10 = 1.0 / math.sqrt(10.0)
    e3 = [
        (rate * (1.0 / 3.0)) * (inv3 * c3[a] - 5.0 * inv * c1[a]) * root10 for a in range(3)
    ]
    h0 = e0 - (3.0 / math.sqrt(6.0)) * e4
    lin = [inv * e1[a] - (5.0 * root10) * inv * e3[a] for a in range(3)]
    qa = e4 * (1.0 / math.sqrt(6.0))
    qb = e8 * 0.5
    qc = e9 * (1.0 / math.sqrt(12.0))
    qd = [inv2 * (qa + qb + qc), inv2 * (qa - qb + qc), inv2 * (qa - 2.0 * qc)]
    qo = [inv2 * eo[k] for k in range(3)]
    cubic = [(root10 * inv3) * e3[a] for a in range(3)]
    tau = cubic[0] * ux + cubic[1] * uy + cubic[2] * uz
    full = {(a, a): 2.0 * qd[a] for a in range(3)}
    for k, (a, b) in enumerate(pairs):
        full[a, b] = full[b, a] = qo[k]
    qu = [full[a, 0] * ux + full[a, 1] * uy + full[a, 2] * uz for a in range(3)]
    constant = (
        h0
        - (lin[0] * ux + lin[1] * uy + lin[2] * uz)
        - tau * u2
        + 0.5 * (qu[0] * ux + qu[1] * uy + qu[2] * uz)
    )
    linear = [lin[a] + u2 * cubic[a] + 2.0 * tau * u[a] - qu[a] for a in range(3)]
    square = [qd[a] - 2.0 * cubic[a] * u[a] - tau for a in range(3)]
    cross = [
        qo[k] - 2.0 * (cubic[a] * u[b] + cubic[b] * u[a]) for k, (a, b) in enumerate(pairs)
    ]
    put_rows([constant] + linear + square + cross + cubic, where, rhs, temp)


def stencil(cells):
    source = lax.broadcasted_iota(jnp.int32, (2 * cells, 2 * cells), 0)
    target = lax.broadcasted_iota(jnp.int32, (2 * cells, 2 * cells), 1)
    source = jnp.where(source >= cells, source - cells, source)
    up = target < cells
    target = jnp.where(up, target, target - cells)
    ahead = jnp.where(up, source - target, target - source)
    ahead = jnp.where(ahead < 0, ahead + cells, ahead)
    values = jnp.where(ahead == 0, 3.0, 0.0) + jnp.where(ahead == 1, -4.0, 0.0)
    return (values + jnp.where(ahead == 2, 1.0, 0.0)).astype(BF16)


def spread_columns(cols, coef):
    block, cells = coef.shape[1:]
    for k in range(6):
        coef[k] = jnp.broadcast_to(cols[:, k : k + 1], (block, cells))


def split2(values):
    high = values.astype(BF16)
    return high, (values - high.astype(F32)).astype(BF16)


def move_y(values, coef, matrix):
    cells = values.shape[1]
    both = mxu(jnp.concatenate(split2(values), axis=1), matrix[...])
    change = jnp.where(coef[5] > 0.0, both[:, :cells], both[:, cells:])
    return values + coef[3] * change


def add_moments(weighted, tab, acc, where):
    high, low = split2(weighted)
    sums = mxu(tab[0 : 2 * GROUP, :], high)
    acc[:, where] = acc[:, where] + (
        sums[0:GROUP] + sums[GROUP : 2 * GROUP] + mxu(tab[0:GROUP, :], low)
    )


def main_kernel(first, step, points, *refs):
    if first:
        macro, field, lhs_e, tab, cols = refs[:5]
        refs = refs[5:]
    else:
        low, high, macro, field, edge_low, edge_high, lhs_r, lhs_e, tab, cols = refs[:10]
        refs = refs[10:]
    out, moments, coef, moved, matrix, rhs_e, acc, temp, parts, heavy = refs[:10]
    if first:
        (turned,) = refs[10:]
    else:
        rhs_r, keep, joint = refs[10:]
    wide = temp.shape[1]
    block, cells = coef.shape[1:]
    chunk = min(16, block)
    rows_x = out.shape[0]
    total = rows_x * cells
    pairs = rows_x // 2
    here, last = pl.program_id(0), pl.num_programs(0) - 1

    @pl.when(here == 0)
    def _():
        temp[...] = jnp.zeros_like(temp)
        matrix[...] = stencil(cells)
        rhs_e[6 * GROUP :, :] = jnp.zeros((128 - 6 * GROUP, total), BF16)
        for edge in (0, 1, rows_x + 2, rows_x + 3):
            moved[edge] = jnp.zeros((block, cells), F32)
        acc[...] = jnp.zeros_like(acc)

        @pl.loop(0, total // wide)
        def _(k):
            where = pl.ds(pl.multiple_of(k * wide, wide), wide)
            exponent_rows(macro, step, where, rhs_e, temp)

        if not first:
            rhs_r[6 * GROUP :, :] = jnp.zeros((128 - 6 * GROUP, total), BF16)
            for p in range(pairs):
                half, q = (low, p) if p < pairs // 2 else (high, p - pairs // 2)
                joint[0:MODES, p * 2 * cells : (p + 1) * 2 * cells] = half[
                    q * MODES : (q + 1) * MODES, :
                ]
            temp[...] = jnp.zeros_like(temp)

            @pl.loop(0, total // wide)
            def _(k):
                where = pl.ds(pl.multiple_of(k * wide, wide), wide)
                spread_rows(macro, step + 1, where, points, joint, rhs_r, keep, temp)

    spread_columns(cols, coef)
    if first:
        for v in range(0, block, 8):
            for x in range(0, rows_x, 8):
                turned[x : x + 8, v : v + 8] = jnp.swapaxes(field[v : v + 8, x : x + 8], 0, 1)
        field = turned

    def layer(x, rows):
        if not first and x < 2:
            return edge_low[x, rows]
        if not first and x >= rows_x - 2:
            return edge_high[x - rows_x + 2, rows]
        return field[x, rows]

    def along_y(p):
        if not first:
            returned = mxu(lhs_r[...], rhs_r[:, p * 2 * cells : (p + 1) * 2 * cells])
        for start in range(0, block, chunk):
            rows = slice(start, start + chunk)
            for k in range(2):
                x = 2 * p + k
                values = layer(x, rows)
                if not first:
                    values = (
                        values * keep[:, x * cells : (x + 1) * cells]
                        + returned[rows, k * cells : (k + 1) * cells]
                    )
                moved[x + 2, rows] = values
                high, low = split2(values)
                both_rows = slice(k * block + start, k * block + start + chunk)
                parts[p % 2, both_rows, 0:cells] = high
                parts[p % 2, both_rows, cells:] = low
        both = mxu(parts[p % 2], matrix[...])
        for start in range(0, block, chunk):
            rows = slice(start, start + chunk)
            up = coef[5, rows] > 0.0
            for k in range(2):
                x = 2 * p + k
                both_rows = slice(k * block + start, k * block + start + chunk)
                change = jnp.where(up, both[both_rows, :cells], both[both_rows, cells:])
                moved[x + 2, rows] = moved[x + 2, rows] + coef[3, rows] * change

    def along_x(p):
        where = slice(p * 2 * cells, (p + 1) * 2 * cells)
        exponent = mxu(lhs_e[...], rhs_e[:, where])
        for start in range(0, block, chunk):
            rows = slice(start, start + chunk)
            line = [moved[2 * p + k, rows] for k in range(6)]
            positive = coef[4, rows] > 0.0
            for k in range(2):
                near = jnp.where(positive, line[k + 3], line[k + 1])
                far = jnp.where(positive, line[k + 4], line[k])
                value = coef[0, rows] * line[k + 2] + coef[1, rows] * near + coef[2, rows] * far
                out[2 * p + k, rows] = value
                high, low = split2(jnp.exp2(exponent[rows, k * cells : (k + 1) * cells]) * value)
                heavy[p % 2, 0, rows, k * cells : (k + 1) * cells] = high
                heavy[p % 2, 1, rows, k * cells : (k + 1) * cells] = low
        sums = mxu(tab[0 : 2 * GROUP, :], heavy[p % 2, 0])
        acc[:, where] = acc[:, where] + (
            sums[0:GROUP] + sums[GROUP : 2 * GROUP] + mxu(tab[0:GROUP, :], heavy[p % 2, 1])
        )

    along_y(0)
    for p in range(pairs):
        if p + 1 < pairs:
            along_y(p + 1)
        along_x(p)

    @pl.when(here == last)
    def _():
        for p in range(pairs):
            where = slice(p * 2 * cells, (p + 1) * 2 * cells)
            side, q = divmod(p, pairs // 2)
            moments[side, q * MODES : (q + 1) * MODES, :] = acc[0:MODES, where]


def whole(shape):
    return pl.BlockSpec(shape, lambda i: (0,) * len(shape))


def main_step(step, points, block, field, macro, tables, summed, edges=None):
    lhs_r, lhs_e, tab, cols = tables
    first = summed is None
    if first:
        count, rows_x, cells = field.shape
        field_spec = pl.BlockSpec((block, rows_x, cells), lambda i: (i, 0, 0))
    else:
        rows_x, count, cells = field.shape
        field_spec = pl.BlockSpec((rows_x, block, cells), lambda i: (0, i, 0))
    total = rows_x * cells
    halves = (rows_x // 4) * MODES
    table_specs = [
        pl.BlockSpec((block, 128), lambda i: (i, 0)),
        pl.BlockSpec((3 * GROUP, block), lambda i: (0, i)),
        pl.BlockSpec((block, 128), lambda i: (i, 0)),
    ]
    if first:
        args = (macro, field, lhs_e, tab, cols)
        specs = [whole(macro.shape), field_spec] + table_specs
    else:
        args = (*summed, macro, field, *edges, lhs_r, lhs_e, tab, cols)
        edge_spec = pl.BlockSpec((2, block, cells), lambda i: (0, i, 0))
        specs = (
            [whole((halves, 2 * cells))] * 2
            + [whole(macro.shape), field_spec, edge_spec, edge_spec, table_specs[0]]
            + table_specs
        )
    scratch = [
        pltpu.VMEM((6, block, cells), F32),
        pltpu.VMEM((rows_x + 4, block, cells), F32),
        pltpu.VMEM((2 * cells, 2 * cells), BF16),
        pltpu.VMEM((128, total), BF16),
        pltpu.VMEM((GROUP, total), F32),
        pltpu.VMEM((GROUP, min(512, total)), F32),
        pltpu.VMEM((2, 2 * block, 2 * cells), BF16),
        pltpu.VMEM((2, 2, block, 2 * cells), BF16),
    ]
    if first:
        scratch += [pltpu.VMEM((rows_x, block, cells), F32)]
    else:
        scratch += [
            pltpu.VMEM((128, total), BF16),
            pltpu.VMEM((1, total), F32),
            pltpu.VMEM((GROUP, total), F32),
        ]
    return pl.pallas_call(
        functools.partial(main_kernel, first, step, points),
        grid=(count // block,),
        in_specs=specs,
        out_specs=[
            pl.BlockSpec((rows_x, block, cells), lambda i: (0, i, 0)),
            whole((2, halves, 2 * cells)),
        ],
        out_shape=[
            jax.ShapeDtypeStruct((rows_x, count, cells), F32),
            jax.ShapeDtypeStruct((2, halves, 2 * cells), F32),
        ],
        scratch_shapes=scratch,
        compiler_params=pltpu.CompilerParams(vmem_limit_bytes=VMEM_LIMIT),
        cost_estimate=pl.CostEstimate(
            flops=20 * count * total, bytes_accessed=8 * count * total, transcendentals=0
        ),
        name="main",
    )(*args)


def edge_kernel(first, step, points, *refs):
    if first:
        macro, before, after, lhs_e, tab, cols, sums, line_low, line_high = refs[:9]
        refs = refs[9:]
    else:
        near_sums, near_macro, macro, before, after = refs[:5]
        lhs_r, lhs_e, tab, cols, sums, line_low, line_high = refs[5:12]
        refs = refs[12:]
    low_out, high_out, sums_low, sums_high, coef, matrix, rhs_e, acc, temp = refs[:9]
    if not first:
        rhs_r, keep = refs[9:]
    block, cells = coef.shape[1:]
    width = 2 * cells
    rows_half = sums.shape[1]
    here = pl.program_id(0)

    @pl.when(here == 0)
    def _():
        temp[...] = jnp.zeros_like(temp)
        matrix[...] = stencil(cells)
        acc[...] = jnp.zeros_like(acc)
        rhs_e[...] = jnp.zeros_like(rhs_e)
        total = macro.shape[2]
        for side in range(2):
            own = slice(side * (total - width), side * (total - width) + width)
            into = slice(side * width, side * width + width)
            exponent_rows(macro, step, own, rhs_e, temp, into)
        if not first:
            temp[...] = jnp.zeros_like(temp)
            rhs_r[...] = jnp.zeros_like(rhs_r)
            spread_rows(
                near_macro, step + 1, slice(0, 2 * width), points, near_sums, rhs_r, keep, temp
            )

    spread_columns(cols, coef)
    sign = coef[4]
    for side, halo in enumerate((before, after)):
        lanes = slice(side * width, side * width + width)
        weight = jnp.exp2(mxu(lhs_e[...], rhs_e[:, lanes]))
        if not first:
            returned = mxu(lhs_r[...], rhs_r[:, lanes])
        moved = []
        for k in range(2):
            values = halo[k]
            if not first:
                lane = slice(k * cells, (k + 1) * cells)
                values = values * keep[:, side * width + k * cells :][:, :cells]
                values = values + returned[:, lane]
            moved.append(move_y(values, coef, matrix))
        if side == 0:
            takes = sign < 0.0
            extra = [coef[1] * moved[1] + coef[2] * moved[0], coef[2] * moved[1]]
        else:
            takes = sign > 0.0
            extra = [coef[2] * moved[0], coef[1] * moved[0] + coef[2] * moved[1]]
        extra = [jnp.where(takes, value, 0.0) for value in extra]
        for k in range(2):
            if side == 0:
                low_out[k] = line_low[k] + extra[k]
            else:
                high_out[k] = line_high[k] + extra[k]
        add_moments(jnp.concatenate(extra, axis=1) * weight, tab, acc, lanes)

    @pl.when(here == pl.num_programs(0) - 1)
    def _():
        sums_low[...] = sums[0]
        sums_high[...] = sums[1]
        sums_low[0:MODES, :] = sums[0, 0:MODES] + acc[0:MODES, 0:width]
        sums_high[rows_half - MODES :, :] = sums[1, rows_half - MODES :] + acc[0:MODES, width:]


def edge_step(step, points, block, halo, line, sums, macro, near, tables, near_sums):
    lhs_r, lhs_e, tab, cols = tables
    first = near_sums is None
    rows_x, count, cells = line.shape
    width = 2 * cells
    by_rows = pl.BlockSpec((block, 128), lambda i: (i, 0))
    by_layers = pl.BlockSpec((2, block, cells), lambda i: (0, i, 0))
    by_columns = pl.BlockSpec((3 * GROUP, block), lambda i: (0, i))
    line_high = pl.BlockSpec((2, block, cells), lambda i: (rows_x // 2 - 1, i, 0))
    args, specs = [macro, *halo], [whole(macro.shape), by_layers, by_layers]
    if not first:
        args = [near_sums, near] + args + [lhs_r]
        specs = [whole(near_sums.shape), whole(near.shape)] + specs + [by_rows]
    args += [lhs_e, tab, cols, sums, line, line]
    specs += [by_rows, by_columns, by_rows, whole(sums.shape), by_layers, line_high]
    scratch = [
        pltpu.VMEM((6, block, cells), F32),
        pltpu.VMEM((width, width), BF16),
        pltpu.VMEM((128, 2 * width), BF16),
        pltpu.VMEM((GROUP, 2 * width), F32),
        pltpu.VMEM((GROUP, 2 * width), F32),
    ]
    if not first:
        scratch += [pltpu.VMEM((128, 2 * width), BF16), pltpu.VMEM((1, 2 * width), F32)]
    return pl.pallas_call(
        functools.partial(edge_kernel, first, step, points),
        grid=(count // block,),
        in_specs=specs,
        out_specs=[by_layers, by_layers] + [whole(sums.shape[1:])] * 2,
        out_shape=[jax.ShapeDtypeStruct((2, count, cells), F32)] * 2
        + [jax.ShapeDtypeStruct(sums.shape[1:], F32)] * 2,
        scratch_shapes=scratch,
        compiler_params=pltpu.CompilerParams(vmem_limit_bytes=VMEM_LIMIT),
        name="edge",
    )(*args)


def last_kernel(
    points, low, high, macro, field, edge_low, edge_high, lhs_r, out, rhs_r, keep, joint, temp, turned
):
    rows_x, block, cells = field.shape
    total = rows_x * cells
    pairs = rows_x // 2
    wide = temp.shape[1]

    @pl.when(pl.program_id(0) == 0)
    def _():
        temp[...] = jnp.zeros_like(temp)
        rhs_r[6 * GROUP :, :] = jnp.zeros((128 - 6 * GROUP, total), BF16)
        for p in range(pairs):
            half, q = (low, p) if p < pairs // 2 else (high, p - pairs // 2)
            joint[0:MODES, p * 2 * cells : (p + 1) * 2 * cells] = half[
                q * MODES : (q + 1) * MODES, :
            ]

        @pl.loop(0, total // wide)
        def _(k):
            where = pl.ds(pl.multiple_of(k * wide, wide), wide)
            spread_rows(macro, 0, where, points, joint, rhs_r, keep, temp)

    for x in range(0, rows_x, 8):
        for p in range(x // 2, x // 2 + 4):
            returned = mxu(lhs_r[...], rhs_r[:, p * 2 * cells : (p + 1) * 2 * cells])
            for k in range(2):
                lane = slice((2 * p + k) * cells, (2 * p + k + 1) * cells)
                if p == 0:
                    values = edge_low[k]
                elif p == pairs - 1:
                    values = edge_high[k]
                else:
                    values = field[2 * p + k]
                turned[2 * p + k - x] = (
                    values * keep[:, lane] + returned[:, k * cells : (k + 1) * cells]
                )
        for v in range(0, block, 8):
            out[v : v + 8, x : x + 8] = jnp.swapaxes(turned[:, v : v + 8], 0, 1)


def last_step(points, block, field, macro, tables, summed, edges):
    rows_x, count, cells = field.shape
    total = rows_x * cells
    halves = (rows_x // 4) * MODES
    return pl.pallas_call(
        functools.partial(last_kernel, points),
        grid=(count // block,),
        in_specs=[whole((halves, 2 * cells))] * 2
        + [
            whole(macro.shape),
            pl.BlockSpec((rows_x, block, cells), lambda i: (0, i, 0)),
            pl.BlockSpec((2, block, cells), lambda i: (0, i, 0)),
            pl.BlockSpec((2, block, cells), lambda i: (0, i, 0)),
            pl.BlockSpec((block, 128), lambda i: (i, 0)),
        ],
        out_specs=pl.BlockSpec((block, rows_x, cells), lambda i: (i, 0, 0)),
        out_shape=jax.ShapeDtypeStruct((count, rows_x, cells), F32),
        scratch_shapes=[
            pltpu.VMEM((128, total), BF16),
            pltpu.VMEM((1, total), F32),
            pltpu.VMEM((GROUP, total), F32),
            pltpu.VMEM((GROUP, min(512, total)), F32),
            pltpu.VMEM((8, block, cells), F32),
        ],
        compiler_params=pltpu.CompilerParams(vmem_limit_bytes=VMEM_LIMIT),
        name="last",
    )(*summed, macro, field, *edges, tables[0])


def sum_over_vel(low, high):
    members = lax.axis_size("vel")
    even = lax.rem(lax.axis_index("vel"), 2) == 0

    def partner(bit):
        return [(i, i ^ bit) for i in range(members)]

    mine = jnp.where(even, low, high)
    mine = mine + lax.ppermute(jnp.where(even, high, low), "vel", partner(1))
    bit = 2
    while bit < members:
        mine = mine + lax.ppermute(mine, "vel", partner(bit))
        bit *= 2
    other = lax.ppermute(mine, "vel", partner(1))
    return jnp.where(even, mine, other), jnp.where(even, other, mine)


def from_sides(to_before, to_after):
    peers = lax.axis_size("space")
    up = [(i, (i + 1) % peers) for i in range(peers)]
    down = [(j, i) for i, j in up]
    return lax.ppermute(to_after, "space", up), lax.ppermute(to_before, "space", down)


def shards(cotangent, speed, direction, macroscopic_record):
    count, rows_x, cells = cotangent.shape
    points = count * lax.axis_size("vel")
    steps = macroscopic_record.shape[0]
    block = min(BLOCK, count)
    width = 2 * cells

    def with_cells(where):
        record = macroscopic_record[:, :, where].reshape(steps * 5, 2, cells)
        record = jnp.pad(record, ((0, -steps * 5 % 8), (0, 0), (0, 0)))
        return jnp.transpose(jnp.concatenate([cotangent[:, where], record]), (1, 0, 2))

    halo = from_sides(with_cells(slice(0, 2)), with_cells(slice(rows_x - 2, rows_x)))
    near = jnp.concatenate(
        [
            jnp.transpose(part[:, count : count + steps * 5], (1, 0, 2)).reshape(steps, 5, width)
            for part in halo
        ],
        axis=2,
    )
    macro = macroscopic_record.reshape(steps, 5, rows_x * cells)
    tables = make_tables(speed, direction)
    field, summed, near_sums, edges = cotangent, None, None, None
    for step in range(steps - 1, -1, -1):
        field, sums = main_step(step, points, block, field, macro, tables, summed, edges)
        *edges, low, high = edge_step(
            step, points, min(256, count), halo, field, sums, macro, near, tables, near_sums
        )
        if step > 0:
            halo = from_sides(*edges)
        summed = sum_over_vel(low, high)
        if step > 0:
            near_sums = jnp.concatenate(
                from_sides(summed[0][:MODES], summed[1][-MODES:]), axis=1
            )
    return last_step(points, min(128, count), field, macro, tables, summed, edges)


def solution(mesh):
    in_specs = (
        P("vel", "space", None),
        P(None, "vel"),
        P(None, "vel"),
        P(None, None, "space", None),
    )
    out_specs = P("vel", "space", None)
    return jax.shard_map(shards, mesh=mesh, in_specs=in_specs, out_specs=out_specs, check_vma=False)
```
